128 devices in a mesh: rep: 4 (over y_hi, core), fsdp: 32 (over z, y_lo, x).
Axes of the slice: x: 4, y: 4 (y_hi: 2, y_lo: 2; y = y_hi * 2 + y_lo), z: 4, core: 2. Of those that a mesh axis runs over, the one named last changes fastest.
Arguments:
- tokens: bfloat16 [16384, 1088], P(('rep', 'fsdp')), may hold values from -6 to 6
- segments: int32 [16384], P(('rep', 'fsdp')), may hold values from 0 to 101, as said below
- ln_gain: bfloat16 [1, 2, 1088], P(None, None, 'fsdp'), may hold values from 0.099609375 to 1.8984375
- ln_bias: bfloat16 [1, 2, 1088], P(None, None, 'fsdp'), may hold values from -1.75 to 1.75
- w_qkv: bfloat16 [1, 1088, 3264], P(None, 'fsdp'), may hold values from -1 to 1
- w_out: bfloat16 [1, 1088, 1088], P(None, 'fsdp'), may hold values from -0.5 to 0.5
- w_fc1: bfloat16 [1, 1088, 4352], P(None, 'fsdp'), may hold values from -0.1875 to 0.1875
- w_fc2: bfloat16 [1, 4352, 1088], P(None, 'fsdp'), may hold values from -0.09375 to 0.09375
- cotangent: bfloat16 [16384, 1088], P(('rep', 'fsdp')), may hold values from -6 to 6
Outputs:
- block_output: bfloat16 [16384, 1088], P(('rep', 'fsdp'))
- grad_tokens: float32 [16384, 1088], P(('rep', 'fsdp'))
- grad_ln_gain: float32 [1, 2, 1088], P(None, None, 'fsdp')
- grad_ln_bias: float32 [1, 2, 1088], P(None, None, 'fsdp')
- grad_qkv: float32 [1, 1088, 3264], P(None, 'fsdp')
- grad_out: float32 [1, 1088, 1088], P(None, 'fsdp')
- grad_fc1: float32 [1, 1088, 4352], P(None, 'fsdp')
- grad_fc2: float32 [1, 4352, 1088], P(None, 'fsdp')
The draws below stay inside these ranges and needn't reach their ends.
Inputs may be any that keep to these rules, and one draw needn't show every extreme that they name: `segments`: segment numbers never fall along the token stream and each number from 0 to the most is used; a document is a run of equal numbers, 20 to 300 tokens long before sequence ends cut it.
All inputs are finite; a program needn't handle non-finite values.
Results may differ from the reference program's by a relative error of at most 0.025.
Values may be sent and summed in bfloat16 or wider, within the bound.
A program may use at most 192 MiB of HBM per device.

```python
import math
import jax
import jax.numpy as jnp
from jax import lax

D = 1088
HEADS = 17
HEAD_DIM = 64
FF = 4352
SEQ = 128
LAYERS = 1
DOC_MIN = 20
DOC_MAX = 300
SEQS = 128
TOKENS = 16384


def draw_segments(key, part):
    stream_len = SEQS * SEQ
    doc_count = stream_len // ((DOC_MIN + DOC_MAX) // 2)
    mean_len = stream_len // doc_count
    jitter_most = min(mean_len - DOC_MIN, DOC_MAX - mean_len - 1) // 2
    jitter = jax.random.randint(key, (doc_count,), -jitter_most, jitter_most + 1)
    keep_jitter = (jnp.arange(doc_count) < doc_count - 1).astype(jnp.int32)
    doc_ends = jnp.arange(1, doc_count + 1) * stream_len // doc_count + jitter * keep_jitter
    positions = jnp.arange(stream_len)
    return jnp.searchsorted(doc_ends, positions, side='right').astype(jnp.int32)


def draw_w_qkv(key, part):
    key_one = jax.random.fold_in(key, 0)
    base_draw = jax.random.normal(key_one, (LAYERS, D, 3 * D), jnp.float32)
    return jnp.clip(base_draw * (1.0 / math.sqrt(D)), -1.0, 1.0).astype(jnp.bfloat16)


def levels(stream_key, extent, cuts, least, top_value):
    level = 1.0
    for dim, shards_of in cuts:
        draws = jax.random.uniform(jax.random.fold_in(jax.random.fold_in(stream_key, 6), dim), (shards_of,), jnp.float32, least / len(cuts), top_value / len(cuts))
        level = level * jnp.repeat(jnp.exp(draws), extent[dim] // shards_of).reshape((-1,) + (1,) * (len(extent) - 1 - dim))
    return level


def scatter_about(stream_key, dims, spread, most, shards=(), kind=jnp.bfloat16):
    drawn = jax.random.normal(stream_key, dims, jnp.float32) * spread
    if len(shards) > 0:
        drawn = levels(stream_key, dims, shards, -0.22, 0.18) * drawn
    return jnp.clip(drawn, min=-most, max=most).astype(kind)


def setup_inputs(seed: int = 0) -> dict:
    key_list = jax.random.split(jax.random.key(seed), 10)
    return {
        "tokens": scatter_about(key_list[0], (TOKENS, D), 1.0, 6.0, ((0, 128),)),
        "segments": draw_segments(jax.random.fold_in(key_list[9], 71), 0),
        "ln_gain": jnp.clip(1.0 + 0.18 * jax.random.normal(key_list[2], (LAYERS, 2, D), jnp.float32), 0.099609375, 1.8984375).astype(jnp.bfloat16),
        "ln_bias": scatter_about(key_list[3], (LAYERS, 2, D), 0.3, 1.75, ((2, 32),)),
        "w_qkv": draw_w_qkv(jax.random.fold_in(key_list[9], 71), 0),
        "w_out": scatter_about(key_list[5], (LAYERS, D, D), (D // 8) ** -0.5, 0.5, ((1, 32),)),
        "w_fc1": scatter_about(key_list[6], (LAYERS, D, FF), D ** -0.5, 0.1875, ((1, 32),)),
        "w_fc2": scatter_about(key_list[7], (LAYERS, FF, D), FF ** -0.5, 0.09375, ((1, 32),)),
        "cotangent": scatter_about(key_list[8], (TOKENS, D), 1.0, 6.0, ((0, 128),)),
    }


EPS = 1e-05

def normalize(resid_in, gain_full, bias_full):
    feat_mean = lax.optimization_barrier(jnp.mean(resid_in, axis=-1, keepdims=True))
    centred = resid_in - feat_mean
    feat_var = lax.optimization_barrier(jnp.mean(centred * centred, axis=-1, keepdims=True))
    return centred * lax.rsqrt(feat_var + EPS) * gain_full + bias_full

def cross_rows(left_op, right_op):
    return lax.dot_general(left_op, right_op, (((0,), (0,)), ((), ())), preferred_element_type=jnp.float32)

def against(left_op, right_op):
    return lax.dot_general(left_op, right_op, (((1,), (1,)), ((), ())), preferred_element_type=jnp.float32)

def product(pattern, left_op, right_op):
    return jnp.einsum(pattern, left_op.astype(jnp.float32), right_op.astype(jnp.float32))

def allowed_mask(seg_block):
    positions = jnp.arange(seg_block.shape[1])
    causal = positions[:, None] >= positions[None, :]
    same_doc = seg_block[:, :, None] == seg_block[:, None, :]
    return (causal[None] & same_doc)[:, None]

def scores_of(query_part, key_part, allowed):
    scores = product('sqhe,skhe->shqk', query_part, key_part) * 0.125
    return jnp.where(allowed, scores, -1e+30)

def forward_layer(resid_in, allowed, gain, bias, w_query, w_proj, w_first, w_second):
    row_count = resid_in.shape[0]
    seq_count = row_count // SEQ
    gain_full = gain.astype(jnp.float32)
    bias_full = bias.astype(jnp.float32)
    normed_one = normalize(resid_in, gain_full[0], bias_full[0]).astype(jnp.bfloat16)
    proj_qkv = jnp.dot(normed_one, w_query, preferred_element_type=jnp.float32).astype(jnp.bfloat16)
    proj_qkv = proj_qkv.reshape(seq_count, SEQ, 3, HEADS, HEAD_DIM)
    scores = scores_of(proj_qkv[:, :, 0], proj_qkv[:, :, 1], allowed)
    row_max = lax.optimization_barrier(jnp.max(scores, axis=-1, keepdims=True))
    log_total = row_max + jnp.log(lax.optimization_barrier(jnp.sum(jnp.exp(scores - row_max), axis=-1, keepdims=True)))
    probs_half = jnp.exp(scores - log_total).astype(jnp.bfloat16)
    heads_out = product('shqk,skhe->sqhe', probs_half, proj_qkv[:, :, 2]).astype(jnp.bfloat16).reshape(row_count, D)
    resid_mid = resid_in + jnp.dot(heads_out, w_proj, preferred_element_type=jnp.float32)
    normed_two = normalize(resid_mid, gain_full[1], bias_full[1]).astype(jnp.bfloat16)
    pre_act = jnp.dot(normed_two, w_first, preferred_element_type=jnp.float32)
    activated = jax.nn.gelu(pre_act, approximate=False).astype(jnp.bfloat16)
    resid_out = resid_mid + jnp.dot(activated, w_second, preferred_element_type=jnp.float32)
    return (resid_out, (resid_in, normed_one, proj_qkv, heads_out, log_total, resid_mid, normed_two, pre_act, activated))

def backward_layer(grad_stream, kept_acts, allowed, gain, bias, w_query, w_proj, w_first, w_second):
    resid_in, normed_one, proj_qkv, heads_out, log_total, resid_mid, normed_two, pre_act, activated = kept_acts
    row_count = grad_stream.shape[0]
    seq_count = row_count // SEQ
    gain_full = gain.astype(jnp.float32)
    bias_full = bias.astype(jnp.float32)
    grad_half = grad_stream.astype(jnp.bfloat16)
    grad_second = cross_rows(activated, grad_half)
    d_activated = against(grad_half, w_second)
    d_preact = jax.vjp(lambda inner_val: jax.nn.gelu(inner_val, approximate=False), pre_act)[1](d_activated)[0]
    d_preact = d_preact.astype(jnp.bfloat16)
    grad_first = cross_rows(normed_two, d_preact)
    d_normed_two = against(d_preact, w_first)
    pullback = jax.vjp(normalize, resid_mid, gain_full[1], bias_full[1])[1]
    d_mid_norm, d_gain_two, d_bias_two = pullback(d_normed_two)
    d_mid = grad_stream + d_mid_norm
    d_mid_half = d_mid.astype(jnp.bfloat16)
    grad_proj = cross_rows(heads_out, d_mid_half)
    d_heads = against(d_mid_half, w_proj).astype(jnp.bfloat16).reshape(seq_count, SEQ, HEADS, HEAD_DIM)
    query_part = proj_qkv[:, :, 0]
    key_part = proj_qkv[:, :, 1]
    value_part = proj_qkv[:, :, 2]
    scores = scores_of(query_part, key_part, allowed)
    probs_full = jnp.exp(scores - log_total)
    probs_half = probs_full.astype(jnp.bfloat16)
    d_value = product('shqk,sqhe->skhe', probs_half, d_heads)
    d_probs = product('sqhe,skhe->shqk', d_heads, value_part)
    heads_four = heads_out.reshape(seq_count, SEQ, HEADS, HEAD_DIM)
    row_delta = lax.optimization_barrier(jnp.sum(d_heads.astype(jnp.float32) * heads_four.astype(jnp.float32), axis=-1))
    row_delta = jnp.transpose(row_delta, (0, 2, 1))[..., None]
    d_scores = (probs_full * (d_probs - row_delta) * 0.125).astype(jnp.bfloat16)
    d_query = product('shqk,skhe->sqhe', d_scores, key_part)
    d_key = product('shqk,sqhe->skhe', d_scores, query_part)
    d_qkv = jnp.stack([d_query, d_key, d_value], axis=2).reshape(row_count, 3 * D).astype(jnp.bfloat16)
    grad_query = cross_rows(normed_one, d_qkv)
    d_normed_one = against(d_qkv, w_query)
    pullback = jax.vjp(normalize, resid_in, gain_full[0], bias_full[0])[1]
    d_in_norm, d_gain_one, d_bias_one = pullback(d_normed_one)
    d_input = d_mid + d_in_norm
    grad_terms = (jnp.stack([d_gain_one, d_gain_two]), jnp.stack([d_bias_one, d_bias_two]), grad_query, grad_proj, grad_first, grad_second)
    return (d_input, grad_terms)

def reference(tokens, segments, ln_gain, ln_bias, w_qkv, w_out, w_fc1, w_fc2, cotangent):
    block_seqs = min(SEQS, 32)
    block_count = SEQS // block_seqs
    row_count = block_seqs * SEQ
    tok_blocks = tokens.reshape(block_count, row_count, D)
    seg_blocks = segments.reshape(block_count, block_seqs, SEQ)
    cot_blocks = cotangent.reshape(block_count, row_count, D)
    zero_set = (jnp.zeros(ln_gain.shape, jnp.float32), jnp.zeros(ln_bias.shape, jnp.float32), jnp.zeros(w_qkv.shape, jnp.float32), jnp.zeros(w_out.shape, jnp.float32), jnp.zeros(w_fc1.shape, jnp.float32), jnp.zeros(w_fc2.shape, jnp.float32))

    def scan_step(totals, inputs):
        tok_block, seg_block, cot_block = inputs
        allowed = allowed_mask(seg_block)
        stream = tok_block.astype(jnp.float32)
        stored = []
        for layer_idx in range(LAYERS):
            stream, kept_acts = forward_layer(stream, allowed, ln_gain[layer_idx], ln_bias[layer_idx], w_qkv[layer_idx], w_out[layer_idx], w_fc1[layer_idx], w_fc2[layer_idx])
            stored.append(kept_acts)
        grad_stream = cot_block.astype(jnp.float32)
        per_layer = [None] * LAYERS
        for layer_idx in reversed(range(LAYERS)):
            grad_stream, grad_terms = backward_layer(grad_stream, stored[layer_idx], allowed, ln_gain[layer_idx], ln_bias[layer_idx], w_qkv[layer_idx], w_out[layer_idx], w_fc1[layer_idx], w_fc2[layer_idx])
            per_layer[layer_idx] = grad_terms
        stacked = tuple((jnp.stack([per_layer[layer_idx][member] for layer_idx in range(LAYERS)]) for member in range(6)))
        totals = tuple((total_old + total_new for total_old, total_new in zip(totals, stacked)))
        return (totals, (stream.astype(jnp.bfloat16), grad_stream))
    totals, (out_blocks, grad_blocks) = lax.scan(scan_step, zero_set, (tok_blocks, seg_blocks, cot_blocks))
    return (out_blocks.reshape(TOKENS, D), grad_blocks.reshape(TOKENS, D), totals[0], totals[1], totals[2], totals[3], totals[4], totals[5])
```

```python
import jax
import jax.numpy as jnp
from jax import lax
from jax.experimental import pallas as pl
from jax.experimental.pallas import tpu as pltpu
from jax.sharding import PartitionSpec as P

D = 1088
FF = 4352
HEADS = 17
HEAD_DIM = 64
SEQ = 128
EPS = 1e-05
WIDE = 8704
LA = 2176
LB = 128
CR = 40
BF = jnp.bfloat16
F32 = jnp.float32
MESH = pl.DeviceIdType.MESH
VMEM = pl.BlockSpec(memory_space=pltpu.VMEM)
HBM = pl.BlockSpec(memory_space=pl.ANY)


class Place:
    def __init__(self):
        rep = lax.axis_index("rep")
        fs = lax.axis_index("fsdp")
        self.core = rep % 2
        self.x = fs % 4
        self.ylo = (fs // 4) % 2
        self.z = fs // 8
        self.y = (rep // 2) * 2 + self.ylo

    def coord(self, dim):
        return {"x": self.x, "y": self.y, "z": self.z}[dim]

    def near(self, dim, step):
        x, y, z = self.x, self.y, self.z
        if dim == "x":
            x = (x + step + 4) % 4
        elif dim == "y":
            y = (y + step + 4) % 4
        else:
            z = (z + step + 4) % 4
        return {"rep": (y // 2) * 2 + self.core, "fsdp": z * 8 + (y % 2) * 4 + x}

    def partner(self):
        return {
            "rep": (self.y // 2) * 2 + 1 - self.core,
            "fsdp": self.z * 8 + self.ylo * 4 + self.x,
        }


def meet(place, dims):
    barrier = pltpu.get_barrier_semaphore()
    count = 1
    pl.semaphore_signal(barrier, inc=1, device_id=place.partner(), device_id_type=MESH)
    for dim in dims:
        for step in (1, -1):
            pl.semaphore_signal(
                barrier, inc=1, device_id=place.near(dim, step), device_id_type=MESH
            )
            count += 1
    pl.semaphore_wait(barrier, count)


ALL = {"z": (0, 4), "y": (0, 2), "x": (0, 4)}


def region(**given):
    out = dict(ALL)
    out.update(given)
    return out


def slices(reg):
    return tuple(pl.ds(*reg[dim]) for dim in "zyx")


GATHER_ORDERS = (("y", "x", "z"), ("y", "z", "x"), ("x", "z", "y"), ("z", "x", "y"))


def gather_kernel(ia, ib, ic, oa, ob, oc, send_sem, recv_sem, pair_send, pair_recv, own_sem):
    place = Place()
    core = place.core
    own = {"z": (place.z, 1), "y": (place.ylo, 1), "x": (place.x, 1)}
    outs = (oa, ob, oc)
    meet(place, "xyz")

    def piece(kind, j, reg):
        zyx = slices(reg)
        if kind == 0:
            return oa.at[zyx + (pl.ds(core * 16, 16), pl.ds(j * LA, LA))]
        if kind == 1:
            return ob.at[zyx + (slice(None), pl.ds(pl.multiple_of((core * 4 + j) * LB, LB), LB))]
        return oc.at[zyx + (core, j)]

    def start_piece(kind, j):
        if kind == 0:
            return ia.at[:, :, :, pl.ds(core * 16, 16), pl.ds(j * LA, LA)]
        if kind == 1:
            return ib.at[:, :, :, :, pl.ds(pl.multiple_of((core * 4 + j) * LB, LB), LB)]
        return ic.at[:, :, :, core, j]

    def half_core(kind, who, reg):
        zyx = slices(reg)
        if kind == 0:
            return oa.at[zyx + (pl.ds(who * 16, 16),)]
        if kind == 1:
            return ob.at[zyx + (slice(None), pl.ds(pl.multiple_of(who * 512, 512), 512))]
        return oc.at[zyx + (who,)]

    def half_in(kind):
        if kind == 0:
            return ia.at[:, :, :, pl.ds(core * 16, 16)]
        if kind == 1:
            return ib.at[:, :, :, :, pl.ds(pl.multiple_of(core * 512, 512), 512)]
        return ic.at[:, :, :, core]

    sent = []

    def pair_copy(kind, src, dst):
        return pltpu.make_async_remote_copy(
            src_ref=src,
            dst_ref=dst,
            send_sem=pair_send.at[kind],
            recv_sem=pair_recv.at[kind],
            device_id=place.partner(),
            device_id_type=MESH,
        )

    def transfer(j, step, way, kind, dim, sign, reg, first):
        ref = piece(kind, j, reg)
        copy = pltpu.make_async_remote_copy(
            src_ref=start_piece(kind, j) if first else ref,
            dst_ref=ref,
            send_sem=send_sem.at[j, step, way, kind],
            recv_sem=recv_sem.at[j, step, way, kind],
            device_id=place.near(dim, sign),
            device_id_type=MESH,
        )
        return copy

    def plan(j):
        steps = []
        held = dict(own)
        order = GATHER_ORDERS[j]
        single = True
        for dim in order:
            if dim == "y":
                other = (1 - place.ylo, 1)
                if single:
                    got = dict(held)
                    got["y"] = other
                    steps.append(
                        [(0, "y", 1, (0,), held, got), (1, "y", -1, (1, 2), held, got)]
                    )
                else:
                    moves = []
                    for way, sign in ((0, 1), (1, -1)):
                        out = dict(held)
                        out["z"] = (2 * way, 2)
                        got = dict(out)
                        got["y"] = other
                        moves.append((way, "y", sign, (0, 1, 2), out, got))
                    steps.append(moves)
            else:
                me = place.coord(dim)

                def at(delta, base):
                    out = dict(base)
                    out[dim] = ((me + delta + 4) % 4, 1)
                    return out

                steps.append(
                    [
                        (0, dim, 1, (0, 1, 2), held, at(-1, held)),
                        (1, dim, -1, (0, 1, 2), held, at(1, held)),
                    ]
                )
                moves = []
                for way, sign in ((0, 1), (1, -1)):
                    base = dict(held)
                    kinds = (0, 1, 2)
                    if single:
                        kinds = ((0,), (1, 2))[way]
                    elif order[0] == "y":
                        base["y"] = (way, 1)
                    else:
                        base[order[0]] = (2 * way, 2)
                    moves.append((way, dim, sign, kinds, at(-sign, base), at(2, base)))
                steps.append(moves)
            held = dict(held)
            held[dim] = ALL[dim]
            single = False
        return steps

    plans = [plan(j) for j in range(4)]

    def start(j, step):
        for way, dim, sign, kinds, out, got in plans[j][step]:
            for kind in kinds:
                copy = transfer(j, step, way, kind, dim, sign, out, step == 0)
                copy.start()
                sent.append(copy)

    def finish(j, step):
        for way, dim, sign, kinds, out, got in plans[j][step]:
            for kind in kinds:
                transfer(j, step, way, kind, dim, sign, got, False).wait_recv()
        for way, dim, sign, kinds, out, got in plans[j][step]:
            for kind in kinds:
                ref = piece(kind, j, got)
                pair_copy(kind, ref, ref).start()

    for j in (2, 3, 0, 1):
        start(j, 0)
    local = []
    for kind in range(3):
        copy = pltpu.make_async_copy(half_in(kind), half_core(kind, core, own), own_sem.at[kind])
        copy.start()
        local.append(copy)
        pair_copy(kind, half_in(kind), half_core(kind, core, own)).start()
    for copy in local:
        copy.wait()
    for ahead, step in ((1, 0), (1, 1), (0, 0), (1, 2), (0, 1), (1, 3), (0, 2), (0, 3)):
        for j in (2, 3) if ahead else (0, 1):
            finish(j, step)
            start(j, step + 1)
    for j in (0, 1, 2, 3):
        finish(j, 4)
    for copy in sent:
        copy.wait_send()
    for kind in range(3):
        mine = half_core(kind, core, ALL)
        theirs = half_core(kind, 1 - core, ALL)
        pair_copy(kind, mine, theirs).wait()


def gather_all(wa, wb, wc):
    return pl.pallas_call(
        gather_kernel,
        out_shape=(
            jax.ShapeDtypeStruct((4, 2, 4, 32, WIDE), BF),
            jax.ShapeDtypeStruct((4, 2, 4, 136, D), BF),
            jax.ShapeDtypeStruct((4, 2, 4, 2, 4, CR, 128), BF),
        ),
        in_specs=[VMEM] * 3,
        out_specs=(HBM,) * 3,
        scratch_shapes=[
            pltpu.SemaphoreType.DMA((4, 5, 2, 3)),
            pltpu.SemaphoreType.DMA((4, 5, 2, 3)),
            pltpu.SemaphoreType.DMA((3,)),
            pltpu.SemaphoreType.DMA((3,)),
            pltpu.SemaphoreType.DMA((3,)),
        ],
        compiler_params=pltpu.CompilerParams(collective_id=0, has_side_effects=True),
        name="weight_gather",
    )(wa, wb, wc)


def swap_kernel(count, *refs):
    mine, theirs, outs = (refs[k * count : (k + 1) * count] for k in range(3))
    send_sem, recv_sem, own_sem = refs[3 * count :]
    place = Place()
    meet(place, "")

    def swap(k, src, slot):
        return pltpu.make_async_remote_copy(
            src_ref=src,
            dst_ref=outs[k].at[slot],
            send_sem=send_sem.at[k],
            recv_sem=recv_sem.at[k],
            device_id=place.partner(),
            device_id_type=MESH,
        )

    kept = [
        pltpu.make_async_copy(mine[k], outs[k].at[place.core], own_sem.at[k]) for k in range(count)
    ]
    for k in range(count):
        swap(k, theirs[k], place.core).start()
        kept[k].start()
    for k in range(count):
        kept[k].wait()
        swap(k, theirs[k], 1 - place.core).wait()


def swap_pair(mine, theirs):
    count = len(mine)
    out = pl.pallas_call(
        lambda *refs: swap_kernel(count, *refs),
        out_shape=tuple(jax.ShapeDtypeStruct((2,) + a.shape, a.dtype) for a in mine),
        in_specs=[VMEM] * (2 * count),
        out_specs=(HBM,) * count,
        scratch_shapes=[pltpu.SemaphoreType.DMA((count,))] * 3,
        compiler_params=pltpu.CompilerParams(collective_id=1, has_side_effects=True),
        name="pair_swap",
    )(*mine, *theirs)
    return [a.reshape((2 * SEQ, a.shape[-1])) for a in out]


PIECES = ((16, LA), (136, LB), (CR, 128))
REDUCE_ORDERS = (("z", "x", "y"), ("x", "z", "y"), ("y", "z", "x"), ("y", "x", "z"))


class Held:
    def __init__(self, pick, dims):
        self.pick = pick
        self.dims = dims

    def at(self, kind, reg):
        zyx = tuple(pl.ds(*reg[dim]) if dim in self.dims else pl.ds(0, 1) for dim in "zyx")
        return self.pick(kind, zyx)


def extents(reg):
    return tuple(reg[dim][1] for dim in "zyx")


def add_into(dst, terms, lead):
    nz, ny, nx = lead

    def body(i, carry):
        idx = (i // (ny * nx), (i // nx) % ny, i % nx)
        total = terms[0][idx].astype(F32)
        for term in terms[1:]:
            total = total + term[idx].astype(F32)
        dst[idx] = total.astype(BF)
        return carry

    lax.fori_loop(0, nz * ny * nx, body, 0)


def reduce_shapes():
    shapes = []
    for j in range(4):
        order = REDUCE_ORDERS[j]
        leads = []
        if order[0] == "y":
            leads.append((4, 1, 4))
            dims = {"z": 4, "y": 1, "x": 4}
            rings = order[1:]
        else:
            dims = {"z": 4, "y": 2, "x": 4}
            rings = order[:2]
        for dim in rings:
            dims[dim] = 1
            full = dict(dims)
            half = dict(dims)
            if order[0] != "y":
                half["y"] = 1
            elif dim == rings[0]:
                half[rings[1]] = 2
            leads += [tuple(half[d] for d in "zyx")] * 2
            leads += [tuple(full[d] for d in "zyx")] * 2
        if order[0] != "y":
            leads.append((1, 1, 1))
        leads += [(1, 1, 1)] * 2
        for lead in leads:
            for piece in PIECES:
                shapes.append(pltpu.VMEM(lead + piece, BF))
    return shapes


BUFFERS = 11 * 3


def reduce_kernel(ga, gb, gc, fa, fb, fc, *scratch):
    place = Place()
    core = place.core
    bufs = scratch[: 4 * BUFFERS]
    send_sem, recv_sem, pair_send, pair_recv = scratch[4 * BUFFERS :]
    meet(place, "xyz")
    sent = []

    def given(j):
        def pick(kind, zyx):
            if kind == 0:
                return ga.at[zyx + (slice(None), pl.ds(j * LA, LA))]
            if kind == 1:
                return gb.at[zyx + (slice(None), pl.ds(j * LB, LB))]
            return gc.at[zyx + (j,)]

        return Held(pick, "zyx")

    class Stream:
        def __init__(self, j):
            self.j = j
            self.next_buf = 0
            self.next_sem = 0
            self.value = given(j)
            self.reg = region()
            self.order = REDUCE_ORDERS[j]

        def buffer(self, dims):
            base = self.j * BUFFERS + 3 * self.next_buf
            self.next_buf += 1
            refs = bufs[base : base + 3]
            return Held(lambda kind, zyx: refs[kind].at[zyx], dims)

        def slot(self):
            self.next_sem += 1
            return self.next_sem - 1

        def copy(self, slot, kind, src, dst, dim, sign):
            return pltpu.make_async_remote_copy(
                src_ref=src,
                dst_ref=dst,
                send_sem=send_sem.at[self.j, slot, kind],
                recv_sem=recv_sem.at[self.j, slot, kind],
                device_id=place.near(dim, sign),
                device_id_type=MESH,
            )

        def send(self, slot, kinds, src, src_reg, dst, dst_reg, dim, sign):
            for kind in kinds:
                copy = self.copy(
                    slot, kind, src.at(kind, src_reg), dst.at(kind, dst_reg), dim, sign
                )
                copy.start()
                sent.append(copy)

        def take(self, slot, kinds, dst, dst_reg, dim, sign):
            for kind in kinds:
                ref = dst.at(kind, dst_reg)
                self.copy(slot, kind, ref, ref, dim, sign).wait_recv()

        def total(self, kinds, dst, reg, *terms):
            for kind in kinds:
                add_into(dst.at(kind, reg), [t.at(kind, reg) for t in terms], extents(reg))

        def wide_y_start(self):
            self.got = self.buffer("zx")
            self.slots = [self.slot(), self.slot()]
            for way, sign in ((0, -1), (1, 1)):
                reg = dict(self.reg)
                reg["z"] = (2 * way, 2)
                out = dict(reg)
                out["y"] = (1 - place.ylo, 1)
                self.send(self.slots[way], (0, 1, 2), self.value, out, self.got, reg, "y", sign)

        def wide_y_finish(self):
            reg = dict(self.reg)
            reg["y"] = (place.ylo, 1)
            for way, sign in ((0, -1), (1, 1)):
                half = dict(reg)
                half["z"] = (2 * way, 2)
                self.take(self.slots[way], (0, 1, 2), self.got, half, "y", sign)
                self.total((0, 1, 2), self.got, half, self.got, self.value)
            self.value = self.got
            self.reg = reg

        def halves(self, base, dim):
            if self.order[0] != "y":
                return [((0, 1, 2), dict(base, y=(way, 1))) for way in (0, 1)]
            other = "x" if dim == "z" else "z"
            if self.reg[other][1] == 4:
                return [((0, 1, 2), dict(base, **{other: (2 * way, 2)})) for way in (0, 1)]
            return [((0,), base), ((1, 2), base)]

        def block(self, dim, delta):
            return dict(self.reg, **{dim: ((place.coord(dim) + delta + 4) % 4, 1)})

        def ring_a(self, dim):
            rest = [d for d in "zyx" if d != dim and self.reg[d][1] > 1]
            self.full_dims = "".join(rest)
            half_dims = self.full_dims
            if self.order[0] != "y":
                half_dims = half_dims.replace("y", "")
            self.relay = []
            for way in (0, 1):
                relay = self.buffer(half_dims)
                self.relay.append(relay)
            self.main = [self.buffer(self.full_dims) for way in (0, 1)]
            self.sa = [self.slot(), self.slot()]
            self.sb = [self.slot(), self.slot()]
            self.sc = [self.slot(), self.slot()]
            for way, sign in ((0, 1), (1, -1)):
                kinds, reg = self.halves(self.block(dim, 2), dim)[way]
                self.send(
                    self.sa[way], kinds, self.value, reg, self.relay[way], self.local(reg, half_dims, way), dim, sign
                )
            for way, sign in ((0, 1), (1, -1)):
                kinds, reg = self.halves(self.block(dim, sign), dim)[1 - way]
                self.send(self.sc[way], kinds, self.value, reg, self.main[way], reg, dim, sign)
            self.half_dims = half_dims

        def local(self, reg, dims, way):
            out = dict(reg)
            for d in dims:
                if reg[d] == (2 * way, 2):
                    out[d] = (0, 2)
            return out

        def ring_b(self, dim):
            for way, sign in ((0, 1), (1, -1)):
                kinds, reg = self.halves(self.block(dim, sign), dim)[way]
                inner = self.local(reg, self.half_dims, way)
                relay = self.relay[way]
                self.take(self.sa[way], kinds, relay, inner, dim, sign)
                for kind in kinds:
                    dst = relay.at(kind, inner)
                    add_into(dst, [dst, self.value.at(kind, reg)], extents(reg))
                self.send(self.sb[way], kinds, relay, inner, self.main[way], reg, dim, sign)

        def ring_end(self, dim):
            mine = self.block(dim, 0)
            parts = self.halves(mine, dim)
            for way, sign in ((0, 1), (1, -1)):
                self.take(self.sc[way], parts[1 - way][0], self.main[way], parts[1 - way][1], dim, sign)
                self.take(self.sb[way], parts[way][0], self.main[way], parts[way][1], dim, sign)
            self.total((0, 1, 2), self.main[0], mine, self.main[0], self.main[1], self.value)
            self.value = self.main[0]
            self.reg = mine

        def last_y_start(self):
            self.got = self.buffer("")
            self.slots = [self.slot(), self.slot()]
            out = dict(self.reg, y=(1 - place.ylo, 1))
            for way, (kinds, sign) in enumerate((((0,), -1), ((1, 2), 1))):
                self.send(self.slots[way], kinds, self.value, out, self.got, out, "y", sign)

        def last_y_finish(self):
            mine = dict(self.reg, y=(place.ylo, 1))
            for way, (kinds, sign) in enumerate((((0,), -1), ((1, 2), 1))):
                self.take(self.slots[way], kinds, self.got, mine, "y", sign)
                self.total(kinds, self.got, mine, self.got, self.value)
            self.value = self.got
            self.reg = mine

        def far_start(self):
            self.passed = self.buffer("")
            self.got = self.buffer("")
            self.slots = [self.slot(), self.slot()]
            for way, (kinds, sign) in enumerate((((0,), 1), ((1, 2), -1))):
                self.send(self.slots[way], kinds, self.value, self.reg, self.passed, self.reg, "y", sign)

        def far_pass(self):
            self.slots2 = [self.slot(), self.slot()]
            for way, (kinds, sign) in enumerate((((0,), 1), ((1, 2), -1))):
                self.take(self.slots[way], kinds, self.passed, self.reg, "y", sign)
                self.send(self.slots2[way], kinds, self.passed, self.reg, self.got, self.reg, "y", sign)

        def far_end(self):
            j = self.j
            for way, (kinds, sign) in enumerate((((0,), 1), ((1, 2), -1))):
                self.take(self.slots2[way], kinds, self.got, self.reg, "y", sign)
            for kind in range(3):
                mine = self.value.at(kind, self.reg)[0, 0, 0].astype(F32)
                both = (mine + self.got.at(kind, self.reg)[0, 0, 0].astype(F32)).astype(BF)
                if kind == 0:
                    fa[core, :, pl.ds(j * LA, LA)] = both
                elif kind == 1:
                    fb[core, :, pl.ds(j * LB, LB)] = both
                else:
                    fc[core, j] = both

    streams = [Stream(j) for j in range(4)]
    late, early = streams[:2], streams[2:]
    for s in late:
        s.ring_a(s.order[0])
    for s in early:
        s.wide_y_start()
    for s in late:
        s.ring_b(s.order[0])
    for s in early:
        s.wide_y_finish()
        s.ring_a(s.order[1])
    for s in late:
        s.ring_end(s.order[0])
        s.ring_a(s.order[1])
    for s in early:
        s.ring_b(s.order[1])
    for s in late:
        s.ring_b(s.order[1])
    for s in early:
        s.ring_end(s.order[1])
        s.ring_a(s.order[2])
    for s in late:
        s.ring_end(s.order[1])
        s.last_y_start()
    for s in early:
        s.ring_b(s.order[2])
    for s in late:
        s.last_y_finish()
        s.far_start()
    for s in early:
        s.ring_end(s.order[2])
        s.far_start()
    for s in late + early:
        s.far_pass()
    for s in late + early:
        s.far_end()
    finals = (fa, fb, fc)
    for kind in range(3):
        ref = finals[kind].at[core]
        pltpu.make_async_remote_copy(
            src_ref=ref,
            dst_ref=ref,
            send_sem=pair_send.at[kind],
            recv_sem=pair_recv.at[kind],
            device_id=place.partner(),
            device_id_type=MESH,
        ).start()
    for copy in sent:
        copy.wait_send()
    for kind in range(3):
        pltpu.make_async_remote_copy(
            src_ref=finals[kind].at[core],
            dst_ref=finals[kind].at[1 - core],
            send_sem=pair_send.at[kind],
            recv_sem=pair_recv.at[kind],
            device_id=place.partner(),
            device_id_type=MESH,
        ).wait()


def reduce_all(ga, gb, gc):
    return pl.pallas_call(
        reduce_kernel,
        out_shape=(
            jax.ShapeDtypeStruct((2, 16, WIDE), BF),
            jax.ShapeDtypeStruct((2, 136, 512), BF),
            jax.ShapeDtypeStruct((2, 4, CR, 128), BF),
        ),
        in_specs=[VMEM] * 3,
        out_specs=(VMEM,) * 3,
        scratch_shapes=reduce_shapes()
        + [
            pltpu.SemaphoreType.DMA((4, 18, 3)),
            pltpu.SemaphoreType.DMA((4, 18, 3)),
            pltpu.SemaphoreType.DMA((3,)),
            pltpu.SemaphoreType.DMA((3,)),
        ],
        compiler_params=pltpu.CompilerParams(
            collective_id=2, has_side_effects=True, vmem_limit_bytes=60 * 1024 * 1024
        ),
        name="grad_reduce",
    )(ga, gb, gc)


def normalize(resid_in, gain_full, bias_full):
    feat_mean = jnp.mean(resid_in, axis=-1, keepdims=True)
    centred = resid_in - feat_mean
    feat_var = jnp.mean(centred * centred, axis=-1, keepdims=True)
    return centred * lax.rsqrt(feat_var + EPS) * gain_full + bias_full


def dot(left, right):
    return jnp.dot(left, right, preferred_element_type=F32)


def cross_rows(left_op, right_op):
    return lax.dot_general(
        left_op, right_op, (((0,), (0,)), ((), ())), preferred_element_type=F32
    )


def against(left_op, right_op):
    return lax.dot_general(
        left_op, right_op, (((1,), (1,)), ((), ())), preferred_element_type=F32
    )


def product(pattern, left_op, right_op):
    return jnp.einsum(pattern, left_op, right_op, preferred_element_type=F32)


def one_hot(feature_of, columns):
    rows = lax.broadcasted_iota(jnp.int32, (D, columns), 0)
    place = lax.broadcasted_iota(jnp.int32, (D, columns), 1)
    return (rows == feature_of(place)).astype(BF)


def gathered_order(p):
    q = p - 1024
    return jnp.where(p < 1024, (p // 32) * 34 + p % 32, (q // 2) * 34 + 32 + q % 2)


def core_order(core):
    def feature_of(p):
        q = p - 512
        return jnp.where(p < 512, (p // 16) * 34 + 16 * core + p % 16, q * 34 + 32 + core)

    return feature_of


def small_block(rows_a, rows_b, norms):
    lead = rows_a.shape[:-2]
    wide = [(0, 0)] * len(lead)
    return jnp.concatenate(
        [
            rows_a,
            jnp.pad(rows_b, wide + [(0, 0), (0, 64)]),
            jnp.pad(norms[..., None, :], wide + [(0, CR - 35), (0, 94)]),
        ],
        axis=-2,
    )


def body(tokens, segments, ln_gain, ln_bias, w_qkv, w_out, w_fc1, w_fc2, cotangent):
    core = lax.axis_index("rep") % 2
    wide = jnp.concatenate([w_fc1[0], w_qkv[0], w_out[0]], axis=1)
    norms = jnp.concatenate([ln_gain[0], ln_bias[0]], axis=0)
    wc = small_block(
        wide[32:].reshape(2, 4, 17, 128),
        w_fc2[0][:, 1024:].reshape(2, 4, 17, 64),
        jnp.broadcast_to(norms, (2, 4, 34)),
    )
    oa, ob, oc = gather_all(
        wide[:32].reshape(1, 1, 1, 32, WIDE),
        w_fc2[0].reshape(1, 1, 1, 136, D),
        wc.reshape(1, 1, 1, 2, 4, CR, 128),
    )
    big = oa.reshape(1024, WIDE)
    oc = oc.reshape(32, 2, 4, CR, 128)
    rest = oc[:, :, :, :17].reshape(64, WIDE)
    second = lax.dynamic_update_slice(
        ob.reshape(FF, D), oc[:, :, :, 17:34, :64].reshape(FF, 64), (0, 1024)
    )
    norms = oc[:, 0, :, 34, :34].transpose(1, 0, 2).reshape(4, D).astype(F32)
    gain, bias = norms[:2], norms[2:]
    cols_first, cols_qkv, cols_out = slice(0, FF), slice(FF, FF + 3 * D), slice(FF + 3 * D, WIDE)
    hot = one_hot(gathered_order, D)

    def forward(rows, cols):
        moved = dot(rows, hot).astype(BF)
        return dot(moved[:, :1024], big[:, cols]) + dot(moved[:, 1024:], rest[:, cols])

    def backward(rows, cols):
        return jnp.concatenate([against(rows, big[:, cols]), against(rows, rest[:, cols])], axis=1)

    def restore(moved):
        head = moved.astype(BF)
        tail = (moved - head.astype(F32)).astype(BF)
        return against(head, hot) + against(tail, hot)

    seg = segments
    positions = jnp.arange(SEQ)
    allowed = ((positions[:, None] >= positions[None, :]) & (seg[:, None] == seg[None, :]))[None]

    resid_in = tokens.astype(F32)
    normed_one, pull_one = jax.vjp(normalize, resid_in, gain[0], bias[0])
    normed_one = normed_one.astype(BF)
    proj = forward(normed_one, cols_qkv).astype(BF).reshape(SEQ, 3, HEADS, HEAD_DIM)
    query, key, value = proj[:, 0], proj[:, 1], proj[:, 2]
    scores = jnp.where(allowed, product("qhe,khe->hqk", query, key) * 0.125, -1e30)
    row_max = jnp.max(scores, axis=-1, keepdims=True)
    log_total = row_max + jnp.log(jnp.sum(jnp.exp(scores - row_max), axis=-1, keepdims=True))
    probs = jnp.exp(scores - log_total)
    probs_half = probs.astype(BF)
    heads_out = product("hqk,khe->qhe", probs_half, value).astype(BF).reshape(SEQ, D)
    resid_mid = resid_in + forward(heads_out, cols_out)
    normed_two, pull_two = jax.vjp(normalize, resid_mid, gain[1], bias[1])
    normed_two = normed_two.astype(BF)
    pre_act = forward(normed_two, cols_first)
    gelu_val, pull_gelu = jax.vjp(lambda v: jax.nn.gelu(v, approximate=False), pre_act)
    activated = gelu_val.astype(BF)
    resid_out = resid_mid + dot(activated, second)

    grad_half = cotangent
    d_preact = pull_gelu(against(grad_half, second))[0].astype(BF)
    d_mid_norm, d_gain_two, d_bias_two = pull_two(restore(backward(d_preact, cols_first)))
    d_mid = cotangent.astype(F32) + d_mid_norm
    d_mid_half = d_mid.astype(BF)
    d_heads = against(backward(d_mid_half, cols_out).astype(BF), hot).astype(BF)
    d_heads = d_heads.reshape(SEQ, HEADS, HEAD_DIM)
    d_value = product("hqk,qhe->khe", probs_half, d_heads)
    d_probs = product("qhe,khe->hqk", d_heads, value)
    heads_four = heads_out.reshape(SEQ, HEADS, HEAD_DIM)
    row_delta = jnp.sum(d_heads.astype(F32) * heads_four.astype(F32), axis=-1).T[..., None]
    d_scores = (probs * (d_probs - row_delta) * 0.125).astype(BF)
    d_query = product("hqk,khe->qhe", d_scores, key)
    d_key = product("hqk,qhe->khe", d_scores, query)
    d_qkv = jnp.stack([d_query, d_key, d_value], axis=1).reshape(SEQ, 3 * D).astype(BF)
    d_in_norm, d_gain_one, d_bias_one = pull_one(restore(backward(d_qkv, cols_qkv)))
    grad_tokens = d_mid + d_in_norm

    def pick(rows, who):
        return dot(rows, one_hot(core_order(who), 544)).astype(BF)

    def pick_columns(rows, who):
        return jnp.concatenate(
            [lax.dynamic_slice(rows, (0, 512 * who), (SEQ, 512)), rows[:, 1024:]], axis=1
        )

    rows_in = (normed_one, heads_out, normed_two)
    both = (d_qkv, d_mid_half, d_preact, activated)
    mine = [pick(r, core) for r in rows_in] + [pick_columns(grad_half, core)] + list(both)
    theirs = [pick(r, 1 - core) for r in rows_in] + [pick_columns(grad_half, 1 - core)] + list(both)
    one, heads, two, cot, t_qkv, t_mid, t_pre, t_act = swap_pair(mine, theirs)
    grad_wide = jnp.concatenate(
        [
            cross_rows(two, t_pre).astype(BF),
            cross_rows(one, t_qkv).astype(BF),
            cross_rows(heads, t_mid).astype(BF),
        ],
        axis=1,
    )
    grad_second = cross_rows(t_act, cot[:, :512]).astype(BF)
    grad_edge = cross_rows(t_act, cot[:, 512:]).astype(BF).reshape(32, 2, 4, 17, 64)
    grad_edge = jnp.where(core == 0, grad_edge[:, 0], grad_edge[:, 1])
    norm_terms = jnp.stack([d_gain_one, d_gain_two, d_bias_one, d_bias_two]).astype(BF)
    small = small_block(
        grad_wide[512:].reshape(32, 4, 17, 128),
        grad_edge,
        norm_terms.reshape(4, 32, 34).transpose(1, 0, 2),
    )
    fa, fb, fc = reduce_all(
        grad_wide[:512].reshape(4, 2, 4, 16, WIDE),
        grad_second.reshape(4, 2, 4, 136, 512),
        small.reshape(4, 2, 4, 4, CR, 128),
    )
    full = jnp.concatenate(
        [fa.reshape(32, WIDE), fc[:, :, :17].reshape(2, WIDE)], axis=0
    ).astype(F32)
    full_second = jnp.concatenate(
        [fb[0], fb[1], fc[:, :, 17:34, :64].reshape(136, 64)], axis=1
    ).astype(F32)
    norm_sums = jnp.sum(fc[:, :, 34, :34].astype(F32), axis=0)
    return (
        resid_out.astype(BF),
        grad_tokens,
        norm_sums[None, :2],
        norm_sums[None, 2:],
        full[None, :, cols_qkv],
        full[None, :, cols_out],
        full[None, :, cols_first],
        full_second[None],
    )


def solution(mesh):
    rows = P(("rep", "fsdp"), None)
    last = P(None, None, "fsdp")
    middle = P(None, "fsdp", None)
    return jax.shard_map(
        body,
        mesh=mesh,
        in_specs=(rows, P(("rep", "fsdp")), last, last, middle, middle, middle, middle, rows),
        out_specs=(rows, rows, last, last, middle, middle, middle, middle),
        check_vma=False,
    )
```

```python
import jax
import jax.numpy as jnp
from jax import lax
from jax.experimental import pallas as pl
from jax.experimental.pallas import tpu as pltpu
from jax.sharding import PartitionSpec as P

D = 1088
FF = 4352
HEADS = 17
HEAD_DIM = 64
SEQ = 128
EPS = 1e-05
WIDE = 8704
LA = 2176
LB = 128
CR = 48
BF = jnp.bfloat16
F32 = jnp.float32
MESH = pl.DeviceIdType.MESH
VMEM = pl.BlockSpec(memory_space=pltpu.VMEM)
HBM = pl.BlockSpec(memory_space=pl.ANY)


class Place:
    def __init__(self):
        rep = lax.axis_index("rep")
        fs = lax.axis_index("fsdp")
        self.core = rep % 2
        self.x = fs % 4
        self.ylo = (fs // 4) % 2
        self.z = fs // 8
        self.y = (rep // 2) * 2 + self.ylo

    def coord(self, dim):
        return {"x": self.x, "y": self.y, "z": self.z}[dim]

    def near(self, dim, step):
        x, y, z = self.x, self.y, self.z
        if dim == "x":
            x = (x + step + 4) % 4
        elif dim == "y":
            y = (y + step + 4) % 4
        else:
            z = (z + step + 4) % 4
        return {"rep": (y // 2) * 2 + self.core, "fsdp": z * 8 + (y % 2) * 4 + x}

    def partner(self):
        return {
            "rep": (self.y // 2) * 2 + 1 - self.core,
            "fsdp": self.z * 8 + self.ylo * 4 + self.x,
        }


def meet(place, dims):
    barrier = pltpu.get_barrier_semaphore()
    count = 1
    pl.semaphore_signal(barrier, inc=1, device_id=place.partner(), device_id_type=MESH)
    for dim in dims:
        for step in (1, -1):
            pl.semaphore_signal(
                barrier, inc=1, device_id=place.near(dim, step), device_id_type=MESH
            )
            count += 1
    pl.semaphore_wait(barrier, count)


ALL = {"z": (0, 4), "y": (0, 2), "x": (0, 4)}


def region(**given):
    out = dict(ALL)
    out.update(given)
    return out


def slices(reg):
    return tuple(pl.ds(*reg[dim]) for dim in "zyx")


GATHER_ORDERS = (("y", "x", "z"), ("y", "z", "x"), ("x", "z", "y"), ("z", "x", "y"))


def gather_kernel(ia, ib, ic, oa, ob, oc, send_sem, recv_sem, pair_send, pair_recv, own_sem):
    place = Place()
    core = place.core
    own = {"z": (place.z, 1), "y": (place.ylo, 1), "x": (place.x, 1)}
    outs = (oa, ob, oc)
    meet(place, "xyz")

    def piece(kind, j, reg):
        zyx = slices(reg)
        if kind == 0:
            return oa.at[zyx + (pl.ds(core * 16, 16), pl.ds(j * LA, LA))]
        if kind == 1:
            return ob.at[zyx + (slice(None), pl.ds(pl.multiple_of((core * 4 + j) * LB, LB), LB))]
        return oc.at[zyx + (core, j)]

    def start_piece(kind, j):
        if kind == 0:
            return ia.at[:, :, :, pl.ds(core * 16, 16), pl.ds(j * LA, LA)]
        if kind == 1:
            return ib.at[:, :, :, :, pl.ds(pl.multiple_of((core * 4 + j) * LB, LB), LB)]
        return ic.at[:, :, :, core, j]

    def half_core(kind, who, reg):
        zyx = slices(reg)
        if kind == 0:
            return oa.at[zyx + (pl.ds(who * 16, 16),)]
        if kind == 1:
            return ob.at[zyx + (slice(None), pl.ds(pl.multiple_of(who * 512, 512), 512))]
        return oc.at[zyx + (who,)]

    def half_in(kind):
        if kind == 0:
            return ia.at[:, :, :, pl.ds(core * 16, 16)]
        if kind == 1:
            return ib.at[:, :, :, :, pl.ds(pl.multiple_of(core * 512, 512), 512)]
        return ic.at[:, :, :, core]

    sent = []

    def pair_copy(kind, src, dst):
        return pltpu.make_async_remote_copy(
            src_ref=src,
            dst_ref=dst,
            send_sem=pair_send.at[kind],
            recv_sem=pair_recv.at[kind],
            device_id=place.partner(),
            device_id_type=MESH,
        )

    def transfer(j, step, way, kind, dim, sign, reg, first):
        ref = piece(kind, j, reg)
        copy = pltpu.make_async_remote_copy(
            src_ref=start_piece(kind, j) if first else ref,
            dst_ref=ref,
            send_sem=send_sem.at[j, step, way, kind],
            recv_sem=recv_sem.at[j, step, way, kind],
            device_id=place.near(dim, sign),
            device_id_type=MESH,
        )
        return copy

    def plan(j):
        steps = []
        held = dict(own)
        order = GATHER_ORDERS[j]
        single = True
        for dim in order:
            if dim == "y":
                other = (1 - place.ylo, 1)
                if single:
                    got = dict(held)
                    got["y"] = other
                    steps.append(
                        [(0, "y", 1, (0,), held, got), (1, "y", -1, (1, 2), held, got)]
                    )
                else:
                    moves = []
                    for way, sign in ((0, 1), (1, -1)):
                        out = dict(held)
                        out["z"] = (2 * way, 2)
                        got = dict(out)
                        got["y"] = other
                        moves.append((way, "y", sign, (0, 1, 2), out, got))
                    steps.append(moves)
            else:
                me = place.coord(dim)

                def at(delta, base):
                    out = dict(base)
                    out[dim] = ((me + delta + 4) % 4, 1)
                    return out

                steps.append(
                    [
                        (0, dim, 1, (0, 1, 2), held, at(-1, held)),
                        (1, dim, -1, (0, 1, 2), held, at(1, held)),
                    ]
                )
                moves = []
                for way, sign in ((0, 1), (1, -1)):
                    base = dict(held)
                    kinds = (0, 1, 2)
                    if single:
                        kinds = ((0,), (1, 2))[way]
                    elif order[0] == "y":
                        base["y"] = (way, 1)
                    else:
                        base[order[0]] = (2 * way, 2)
                    moves.append((way, dim, sign, kinds, at(-sign, base), at(2, base)))
                steps.append(moves)
            held = dict(held)
            held[dim] = ALL[dim]
            single = False
        return steps

    plans = [plan(j) for j in range(4)]

    def start(j, step):
        for way, dim, sign, kinds, out, got in plans[j][step]:
            for kind in kinds:
                copy = transfer(j, step, way, kind, dim, sign, out, step == 0)
                copy.start()
                sent.append(copy)

    def finish(j, step):
        for way, dim, sign, kinds, out, got in plans[j][step]:
            for kind in kinds:
                transfer(j, step, way, kind, dim, sign, got, False).wait_recv()
        for way, dim, sign, kinds, out, got in plans[j][step]:
            for kind in kinds:
                ref = piece(kind, j, got)
                pair_copy(kind, ref, ref).start()

    for j in (2, 3, 0, 1):
        start(j, 0)
    local = []
    for kind in range(3):
        copy = pltpu.make_async_copy(half_in(kind), half_core(kind, core, own), own_sem.at[kind])
        copy.start()
        local.append(copy)
        pair_copy(kind, half_in(kind), half_core(kind, core, own)).start()
    for copy in local:
        copy.wait()
    for ahead, step in ((1, 0), (1, 1), (0, 0), (1, 2), (0, 1), (1, 3), (0, 2), (0, 3)):
        for j in (2, 3) if ahead else (0, 1):
            finish(j, step)
            start(j, step + 1)
    for j in (0, 1, 2, 3):
        finish(j, 4)
    for copy in sent:
        copy.wait_send()
    for kind in range(3):
        mine = half_core(kind, core, ALL)
        theirs = half_core(kind, 1 - core, ALL)
        pair_copy(kind, mine, theirs).wait()


def gather_all(wa, wb, wc):
    return pl.pallas_call(
        gather_kernel,
        out_shape=(
            jax.ShapeDtypeStruct((4, 2, 4, 32, WIDE), BF),
            jax.ShapeDtypeStruct((4, 2, 4, 136, D), BF),
            jax.ShapeDtypeStruct((4, 2, 4, 2, 4, CR, 128), BF),
        ),
        in_specs=[VMEM] * 3,
        out_specs=(HBM,) * 3,
        scratch_shapes=[
            pltpu.SemaphoreType.DMA((4, 5, 2, 3)),
            pltpu.SemaphoreType.DMA((4, 5, 2, 3)),
            pltpu.SemaphoreType.DMA((3,)),
            pltpu.SemaphoreType.DMA((3,)),
            pltpu.SemaphoreType.DMA((3,)),
        ],
        compiler_params=pltpu.CompilerParams(collective_id=0, has_side_effects=True),
        name="weight_gather",
    )(wa, wb, wc)


def swap_kernel(count, across, *refs):
    mine, theirs, outs = (refs[k * count : (k + 1) * count] for k in range(3))
    send_sem, recv_sem, own_sem = refs[3 * count :]
    place = Place()
    meet(place, "")

    def part(k, who):
        if k < across:
            return outs[k].at[:, pl.ds(pl.multiple_of(who * SEQ, SEQ), SEQ)]
        return outs[k].at[pl.ds(pl.multiple_of(who * SEQ, SEQ), SEQ)]

    def swap(k, who):
        return pltpu.make_async_remote_copy(
            src_ref=theirs[k],
            dst_ref=part(k, who),
            send_sem=send_sem.at[k],
            recv_sem=recv_sem.at[k],
            device_id=place.partner(),
            device_id_type=MESH,
        )

    kept = [
        pltpu.make_async_copy(mine[k], part(k, place.core), own_sem.at[k]) for k in range(count)
    ]
    for k in range(count):
        swap(k, place.core).start()
        kept[k].start()
    for k in range(count):
        kept[k].wait()
        swap(k, 1 - place.core).wait()


def swap_pair(across, mine, theirs):
    count = len(mine)
    return pl.pallas_call(
        lambda *refs: swap_kernel(count, across, *refs),
        out_shape=tuple(
            jax.ShapeDtypeStruct(
                (a.shape[0], 2 * SEQ) if k < across else (2 * SEQ, a.shape[1]), a.dtype
            )
            for k, a in enumerate(mine)
        ),
        in_specs=[VMEM] * (2 * count),
        out_specs=(HBM,) * count,
        scratch_shapes=[pltpu.SemaphoreType.DMA((count,))] * 3,
        compiler_params=pltpu.CompilerParams(collective_id=1, has_side_effects=True),
        name="pair_swap",
    )(*mine, *theirs)


def weight_products(
    one, heads, two, act, pre, mid, tail, last, cot, norms, ga, gb, gc, rows, edge
):
    core = lax.axis_index("rep") % 2
    rows[...] = jnp.zeros_like(rows)
    for j in range(4):
        if j < 2:
            terms = [(two, pre.at[:, pl.ds(j * LA, LA)])]
        elif j == 2:
            terms = [(one, mid)]
        else:
            terms = [(one, tail), (heads, last)]

        def product_of(start, size):
            total = dot(terms[0][0][pl.ds(start, size), :], terms[0][1][...])
            for left, right in terms[1:]:
                total = total + dot(left[pl.ds(start, size), :], right[...])
            return total

        @pl.loop(0, 4)
        def _(z):
            val = product_of(pl.multiple_of(z * 128, 128), 128).astype(BF)
            ga[z, :, :, :, pl.ds(j * LA, LA)] = val.reshape(2, 4, 16, LA)

        val = product_of(512, 32)
        for t in range(17):
            rows[:, t, :] = val[:, t * 128 : (t + 1) * 128]
        rows[:, 17, :] = norms[j]

        @pl.loop(0, 32)
        def _(s):
            gc[s // 8, (s // 4) % 2, s % 4, j, pl.ds(0, 24), :] = rows[s].astype(BF)

    @pl.loop(0, 32)
    def _(s):
        val = dot(act[pl.ds(pl.multiple_of(s * 136, 8), 136), :], cot[...])
        gb[s // 8, (s // 4) % 2, s % 4] = val[:, :512].astype(BF)
        edge[...] = val[:, 512:]
        for j in range(4):
            part = edge[pl.ds(pl.multiple_of(64 * core + 16 * j, 8), 24), :]
            gc[s // 8, (s // 4) % 2, s % 4, j, pl.ds(24, 24), :] = part.astype(BF)


def weight_grads(*operands):
    return pl.pallas_call(
        weight_products,
        out_shape=(
            jax.ShapeDtypeStruct((4, 2, 4, 16, WIDE), BF),
            jax.ShapeDtypeStruct((4, 2, 4, 136, 512), BF),
            jax.ShapeDtypeStruct((4, 2, 4, 4, CR, 128), BF),
        ),
        in_specs=[VMEM] * len(operands),
        out_specs=(VMEM,) * 3,
        scratch_shapes=[pltpu.VMEM((32, 24, 128), F32), pltpu.VMEM((136, 128), F32)],
        compiler_params=pltpu.CompilerParams(vmem_limit_bytes=48 * 1024 * 1024),
        name="weight_grads",
    )(*operands)


PIECES = ((16, LA), (136, LB), (CR, 128))
REDUCE_ORDERS = (("z", "x", "y"), ("x", "z", "y"), ("y", "z", "x"), ("y", "x", "z"))


class Held:
    def __init__(self, pick, dims):
        self.pick = pick
        self.dims = dims

    def at(self, kind, reg):
        zyx = tuple(pl.ds(*reg[dim]) if dim in self.dims else pl.ds(0, 1) for dim in "zyx")
        return self.pick(kind, zyx)


def extents(reg):
    return tuple(reg[dim][1] for dim in "zyx")


def add_into(dst, terms, lead):
    nz, ny, nx = lead

    def body(i, carry):
        idx = (i // (ny * nx), (i // nx) % ny, i % nx)
        total = terms[0][idx].astype(F32)
        for term in terms[1:]:
            total = total + term[idx].astype(F32)
        dst[idx] = total.astype(BF)
        return carry

    lax.fori_loop(0, nz * ny * nx, body, 0)


def reduce_shapes():
    shapes = []
    for j in range(4):
        order = REDUCE_ORDERS[j]
        leads = []
        if order[0] == "y":
            leads.append((4, 1, 4))
            dims = {"z": 4, "y": 1, "x": 4}
            rings = order[1:]
        else:
            dims = {"z": 4, "y": 2, "x": 4}
            rings = order[:2]
        for dim in rings:
            dims[dim] = 1
            full = dict(dims)
            half = dict(dims)
            if order[0] != "y":
                half["y"] = 1
            elif dim == rings[0]:
                half[rings[1]] = 2
            leads += [tuple(half[d] for d in "zyx")] * 2
            leads += [tuple(full[d] for d in "zyx")] * 2
        if order[0] != "y":
            leads.append((1, 1, 1))
        leads += [(1, 1, 1)] * 2
        for lead in leads:
            for piece in PIECES:
                shapes.append(pltpu.VMEM(lead + piece, BF))
    return shapes


BUFFERS = 11 * 3


def reduce_kernel(ga, gb, gc, fa, fb, fc, *scratch):
    place = Place()
    core = place.core
    bufs = scratch[: 4 * BUFFERS]
    send_sem, recv_sem, pair_send, pair_recv = scratch[4 * BUFFERS :]
    meet(place, "xyz")
    sent = []

    def given(j):
        def pick(kind, zyx):
            if kind == 0:
                return ga.at[zyx + (slice(None), pl.ds(j * LA, LA))]
            if kind == 1:
                return gb.at[zyx + (slice(None), pl.ds(j * LB, LB))]
            return gc.at[zyx + (j,)]

        return Held(pick, "zyx")

    class Stream:
        def __init__(self, j):
            self.j = j
            self.next_buf = 0
            self.next_sem = 0
            self.value = given(j)
            self.reg = region()
            self.order = REDUCE_ORDERS[j]

        def buffer(self, dims):
            base = self.j * BUFFERS + 3 * self.next_buf
            self.next_buf += 1
            refs = bufs[base : base + 3]
            return Held(lambda kind, zyx: refs[kind].at[zyx], dims)

        def slot(self):
            self.next_sem += 1
            return self.next_sem - 1

        def copy(self, slot, kind, src, dst, dim, sign):
            return pltpu.make_async_remote_copy(
                src_ref=src,
                dst_ref=dst,
                send_sem=send_sem.at[self.j, slot, kind],
                recv_sem=recv_sem.at[self.j, slot, kind],
                device_id=place.near(dim, sign),
                device_id_type=MESH,
            )

        def send(self, slot, kinds, src, src_reg, dst, dst_reg, dim, sign):
            for kind in kinds:
                copy = self.copy(
                    slot, kind, src.at(kind, src_reg), dst.at(kind, dst_reg), dim, sign
                )
                copy.start()
                sent.append(copy)

        def take(self, slot, kinds, dst, dst_reg, dim, sign):
            for kind in kinds:
                ref = dst.at(kind, dst_reg)
                self.copy(slot, kind, ref, ref, dim, sign).wait_recv()

        def total(self, kinds, dst, reg, *terms):
            for kind in kinds:
                add_into(dst.at(kind, reg), [t.at(kind, reg) for t in terms], extents(reg))

        def wide_y_start(self):
            self.got = self.buffer("zx")
            self.slots = [self.slot(), self.slot()]
            for way, sign in ((0, -1), (1, 1)):
                reg = dict(self.reg)
                reg["z"] = (2 * way, 2)
                out = dict(reg)
                out["y"] = (1 - place.ylo, 1)
                self.send(self.slots[way], (0, 1, 2), self.value, out, self.got, reg, "y", sign)

        def wide_y_finish(self):
            reg = dict(self.reg)
            reg["y"] = (place.ylo, 1)
            for way, sign in ((0, -1), (1, 1)):
                half = dict(reg)
                half["z"] = (2 * way, 2)
                self.take(self.slots[way], (0, 1, 2), self.got, half, "y", sign)
                self.total((0, 1, 2), self.got, half, self.got, self.value)
            self.value = self.got
            self.reg = reg

        def halves(self, base, dim):
            if self.order[0] != "y":
                return [((0, 1, 2), dict(base, y=(way, 1))) for way in (0, 1)]
            other = "x" if dim == "z" else "z"
            if self.reg[other][1] == 4:
                return [((0, 1, 2), dict(base, **{other: (2 * way, 2)})) for way in (0, 1)]
            return [((0,), base), ((1, 2), base)]

        def block(self, dim, delta):
            return dict(self.reg, **{dim: ((place.coord(dim) + delta + 4) % 4, 1)})

        def ring_a(self, dim):
            rest = [d for d in "zyx" if d != dim and self.reg[d][1] > 1]
            self.full_dims = "".join(rest)
            half_dims = self.full_dims
            if self.order[0] != "y":
                half_dims = half_dims.replace("y", "")
            self.relay = []
            for way in (0, 1):
                relay = self.buffer(half_dims)
                self.relay.append(relay)
            self.main = [self.buffer(self.full_dims) for way in (0, 1)]
            self.sa = [self.slot(), self.slot()]
            self.sb = [self.slot(), self.slot()]
            self.sc = [self.slot(), self.slot()]
            for way, sign in ((0, 1), (1, -1)):
                kinds, reg = self.halves(self.block(dim, 2), dim)[way]
                self.send(
                    self.sa[way], kinds, self.value, reg, self.relay[way], self.local(reg, half_dims, way), dim, sign
                )
            for way, sign in ((0, 1), (1, -1)):
                kinds, reg = self.halves(self.block(dim, sign), dim)[1 - way]
                self.send(self.sc[way], kinds, self.value, reg, self.main[way], reg, dim, sign)
            self.half_dims = half_dims

        def local(self, reg, dims, way):
            out = dict(reg)
            for d in dims:
                if reg[d] == (2 * way, 2):
                    out[d] = (0, 2)
            return out

        def ring_b(self, dim):
            for way, sign in ((0, 1), (1, -1)):
                kinds, reg = self.halves(self.block(dim, sign), dim)[way]
                inner = self.local(reg, self.half_dims, way)
                relay = self.relay[way]
                self.take(self.sa[way], kinds, relay, inner, dim, sign)
                for kind in kinds:
                    dst = relay.at(kind, inner)
                    add_into(dst, [dst, self.value.at(kind, reg)], extents(reg))
                self.send(self.sb[way], kinds, relay, inner, self.main[way], reg, dim, sign)

        def ring_end(self, dim):
            mine = self.block(dim, 0)
            parts = self.halves(mine, dim)
            for way, sign in ((0, 1), (1, -1)):
                self.take(self.sc[way], parts[1 - way][0], self.main[way], parts[1 - way][1], dim, sign)
                self.take(self.sb[way], parts[way][0], self.main[way], parts[way][1], dim, sign)
            self.total((0, 1, 2), self.main[0], mine, self.main[0], self.main[1], self.value)
            self.value = self.main[0]
            self.reg = mine

        def last_y_start(self):
            self.got = self.buffer("")
            self.slots = [self.slot(), self.slot()]
            out = dict(self.reg, y=(1 - place.ylo, 1))
            for way, (kinds, sign) in enumerate((((0,), -1), ((1, 2), 1))):
                self.send(self.slots[way], kinds, self.value, out, self.got, out, "y", sign)

        def last_y_finish(self):
            mine = dict(self.reg, y=(place.ylo, 1))
            for way, (kinds, sign) in enumerate((((0,), -1), ((1, 2), 1))):
                self.take(self.slots[way], kinds, self.got, mine, "y", sign)
                self.total(kinds, self.got, mine, self.got, self.value)
            self.value = self.got
            self.reg = mine

        def far_start(self):
            self.passed = self.buffer("")
            self.got = self.buffer("")
            self.slots = [self.slot(), self.slot()]
            for way, (kinds, sign) in enumerate((((0,), 1), ((1, 2), -1))):
                self.send(self.slots[way], kinds, self.value, self.reg, self.passed, self.reg, "y", sign)

        def far_pass(self):
            self.slots2 = [self.slot(), self.slot()]
            for way, (kinds, sign) in enumerate((((0,), 1), ((1, 2), -1))):
                self.take(self.slots[way], kinds, self.passed, self.reg, "y", sign)
                self.send(self.slots2[way], kinds, self.passed, self.reg, self.got, self.reg, "y", sign)

        def far_end(self):
            j = self.j
            for way, (kinds, sign) in enumerate((((0,), 1), ((1, 2), -1))):
                self.take(self.slots2[way], kinds, self.got, self.reg, "y", sign)
            for kind in range(3):
                mine = self.value.at(kind, self.reg)[0, 0, 0].astype(F32)
                both = (mine + self.got.at(kind, self.reg)[0, 0, 0].astype(F32)).astype(BF)
                if kind == 0:
                    fa[core, :, pl.ds(j * LA, LA)] = both
                elif kind == 1:
                    fb[core, :, pl.ds(j * LB, LB)] = both
                else:
                    fc[core, j] = both

    streams = [Stream(j) for j in range(4)]
    late, early = streams[:2], streams[2:]
    for s in late:
        s.ring_a(s.order[0])
    for s in early:
        s.wide_y_start()
    for s in late:
        s.ring_b(s.order[0])
    for s in early:
        s.wide_y_finish()
        s.ring_a(s.order[1])
    for s in late:
        s.ring_end(s.order[0])
        s.ring_a(s.order[1])
    for s in early:
        s.ring_b(s.order[1])
    for s in late:
        s.ring_b(s.order[1])
    for s in early:
        s.ring_end(s.order[1])
        s.ring_a(s.order[2])
    for s in late:
        s.ring_end(s.order[1])
        s.last_y_start()
    for s in early:
        s.ring_b(s.order[2])
    for s in late:
        s.last_y_finish()
        s.far_start()
    for s in early:
        s.ring_end(s.order[2])
        s.far_start()
    for s in late + early:
        s.far_pass()
    for s in late + early:
        s.far_end()
    finals = (fa, fb, fc)
    for kind in range(3):
        ref = finals[kind].at[core]
        pltpu.make_async_remote_copy(
            src_ref=ref,
            dst_ref=ref,
            send_sem=pair_send.at[kind],
            recv_sem=pair_recv.at[kind],
            device_id=place.partner(),
            device_id_type=MESH,
        ).start()
    for copy in sent:
        copy.wait_send()
    for kind in range(3):
        pltpu.make_async_remote_copy(
            src_ref=finals[kind].at[core],
            dst_ref=finals[kind].at[1 - core],
            send_sem=pair_send.at[kind],
            recv_sem=pair_recv.at[kind],
            device_id=place.partner(),
            device_id_type=MESH,
        ).wait()


def reduce_all(ga, gb, gc):
    return pl.pallas_call(
        reduce_kernel,
        out_shape=(
            jax.ShapeDtypeStruct((2, 16, WIDE), BF),
            jax.ShapeDtypeStruct((2, 136, 512), BF),
            jax.ShapeDtypeStruct((2, 4, CR, 128), BF),
        ),
        in_specs=[VMEM] * 3,
        out_specs=(VMEM,) * 3,
        scratch_shapes=reduce_shapes()
        + [
            pltpu.SemaphoreType.DMA((4, 18, 3)),
            pltpu.SemaphoreType.DMA((4, 18, 3)),
            pltpu.SemaphoreType.DMA((3,)),
            pltpu.SemaphoreType.DMA((3,)),
        ],
        compiler_params=pltpu.CompilerParams(
            collective_id=2, has_side_effects=True, vmem_limit_bytes=60 * 1024 * 1024
        ),
        name="grad_reduce",
    )(ga, gb, gc)


def normalize(resid_in, gain_full, bias_full):
    feat_mean = jnp.mean(resid_in, axis=-1, keepdims=True)
    centred = resid_in - feat_mean
    feat_var = jnp.mean(centred * centred, axis=-1, keepdims=True)
    return centred * lax.rsqrt(feat_var + EPS) * gain_full + bias_full


def dot(left, right):
    return jnp.dot(left, right, preferred_element_type=F32)


def cross_rows(left_op, right_op):
    return lax.dot_general(
        left_op, right_op, (((0,), (0,)), ((), ())), preferred_element_type=F32
    )


def against(left_op, right_op):
    return lax.dot_general(
        left_op, right_op, (((1,), (1,)), ((), ())), preferred_element_type=F32
    )


def product(pattern, left_op, right_op):
    return jnp.einsum(pattern, left_op, right_op, preferred_element_type=F32)


def one_hot(feature_of, columns):
    rows = lax.broadcasted_iota(jnp.int32, (D, columns), 0)
    place = lax.broadcasted_iota(jnp.int32, (D, columns), 1)
    return (rows == feature_of(place)).astype(BF)


def gathered_order(p):
    q = p - 1024
    return jnp.where(p < 1024, (p // 32) * 34 + p % 32, (q // 2) * 34 + 32 + q % 2)


def core_order(core):
    def feature_of(p):
        q = p - 512
        return jnp.where(p < 512, (p // 16) * 34 + 16 * core + p % 16, q * 34 + 32 + core)

    return feature_of


def small_block(rows_a, edge, norms):
    pieces = [edge[16 * k : 16 * k + 24] for k in range(8)]
    edges = jnp.stack(pieces).reshape(2, 4, 24, 64)
    norm_rows = jnp.broadcast_to(norms[None, :, None, :], (2, 4, 1, 34))
    return jnp.concatenate(
        [
            rows_a,
            jnp.pad(norm_rows, ((0, 0), (0, 0), (0, 6), (0, 94))),
            jnp.pad(edges, ((0, 0), (0, 0), (0, 0), (0, 64))),
        ],
        axis=2,
    )


def edge_of(small):
    lead = small.shape[:-4]
    return jnp.concatenate(
        [small[..., 24:40, :64].reshape(lead + (128, 64)), small[..., 1, 3, 40:48, :64]], axis=-2
    )


def body(tokens, segments, ln_gain, ln_bias, w_qkv, w_out, w_fc1, w_fc2, cotangent):
    core = lax.axis_index("rep") % 2
    wide = jnp.concatenate([w_fc1[0], w_qkv[0], w_out[0]], axis=1)
    norms = jnp.concatenate([ln_gain[0], ln_bias[0]], axis=0)
    wc = small_block(
        wide[32:].reshape(2, 4, 17, 128),
        w_fc2[0][:, 1024:],
        norms,
    )
    oa, ob, oc = gather_all(
        wide[:32].reshape(1, 1, 1, 32, WIDE),
        w_fc2[0].reshape(1, 1, 1, 136, D),
        wc.reshape(1, 1, 1, 2, 4, CR, 128),
    )
    big = oa.reshape(1024, WIDE)
    oc = oc.reshape(32, 2, 4, CR, 128)
    rest = oc[:, :, :, :17].reshape(64, WIDE)
    second = lax.dynamic_update_slice(
        ob.reshape(FF, D), edge_of(oc).reshape(FF, 64), (0, 1024)
    )
    norms = oc[:, 0, :, 17, :34].transpose(1, 0, 2).reshape(4, D).astype(F32)
    gain, bias = norms[:2], norms[2:]
    cols_first, cols_qkv, cols_out = slice(0, FF), slice(FF, FF + 3 * D), slice(FF + 3 * D, WIDE)
    hot = one_hot(gathered_order, D)

    def forward(rows, cols):
        moved = dot(rows, hot).astype(BF)
        return dot(moved[:, :1024], big[:, cols]) + dot(moved[:, 1024:], rest[:, cols])

    def backward(rows, cols):
        return jnp.concatenate([against(rows, big[:, cols]), against(rows, rest[:, cols])], axis=1)

    def restore(moved):
        head = moved.astype(BF)
        tail = (moved - head.astype(F32)).astype(BF)
        return against(head, hot) + against(tail, hot)

    seg = segments
    positions = jnp.arange(SEQ)
    allowed = ((positions[:, None] >= positions[None, :]) & (seg[:, None] == seg[None, :]))[None]

    resid_in = tokens.astype(F32)
    normed_one, pull_one = jax.vjp(normalize, resid_in, gain[0], bias[0])
    normed_one = normed_one.astype(BF)
    proj = forward(normed_one, cols_qkv).astype(BF).reshape(SEQ, 3, HEADS, HEAD_DIM)
    query, key, value = proj[:, 0], proj[:, 1], proj[:, 2]
    scores = jnp.where(allowed, product("qhe,khe->hqk", query, key) * 0.125, -1e30)
    row_max = jnp.max(scores, axis=-1, keepdims=True)
    log_total = row_max + jnp.log(jnp.sum(jnp.exp(scores - row_max), axis=-1, keepdims=True))
    probs = jnp.exp(scores - log_total)
    probs_half = probs.astype(BF)
    heads_out = product("hqk,khe->qhe", probs_half, value).astype(BF).reshape(SEQ, D)
    resid_mid = resid_in + forward(heads_out, cols_out)
    normed_two, pull_two = jax.vjp(normalize, resid_mid, gain[1], bias[1])
    normed_two = normed_two.astype(BF)
    pre_act = forward(normed_two, cols_first)
    gelu_val, pull_gelu = jax.vjp(lambda v: jax.nn.gelu(v, approximate=False), pre_act)
    activated = gelu_val.astype(BF)
    resid_out = resid_mid + dot(activated, second)

    grad_half = cotangent
    d_preact = pull_gelu(against(grad_half, second))[0].astype(BF)
    d_mid_norm, d_gain_two, d_bias_two = pull_two(restore(backward(d_preact, cols_first)))
    d_mid = cotangent.astype(F32) + d_mid_norm
    d_mid_half = d_mid.astype(BF)
    d_heads = against(backward(d_mid_half, cols_out).astype(BF), hot).astype(BF)
    d_heads = d_heads.reshape(SEQ, HEADS, HEAD_DIM)
    d_value = product("hqk,qhe->khe", probs_half, d_heads)
    d_probs = product("qhe,khe->hqk", d_heads, value)
    heads_four = heads_out.reshape(SEQ, HEADS, HEAD_DIM)
    row_delta = jnp.sum(d_heads.astype(F32) * heads_four.astype(F32), axis=-1).T[..., None]
    d_scores = (probs * (d_probs - row_delta) * 0.125).astype(BF)
    d_query = product("hqk,khe->qhe", d_scores, key)
    d_key = product("hqk,qhe->khe", d_scores, query)
    d_qkv = jnp.stack([d_query, d_key, d_value], axis=1).reshape(SEQ, 3 * D).astype(BF)
    d_in_norm, d_gain_one, d_bias_one = pull_one(restore(backward(d_qkv, cols_qkv)))
    grad_tokens = d_mid + d_in_norm

    def pick(rows, who):
        hot_core = one_hot(core_order(who), 544)
        return lax.dot_general(
            hot_core, rows, (((0,), (1,)), ((), ())), preferred_element_type=F32
        ).astype(BF)

    def pick_columns(rows, who):
        return jnp.concatenate(
            [
                lax.dynamic_slice(rows, (0, 512 * who), (SEQ, 512)),
                jnp.pad(rows[:, 1024:], ((0, 0), (0, 64))),
            ],
            axis=1,
        )

    lefts = (normed_one, heads_out, normed_two)
    same = [
        activated.T,
        d_preact,
        d_qkv[:, :LA],
        jnp.pad(d_qkv[:, LA:], ((0, 0), (0, D))),
        jnp.pad(d_mid_half, ((0, 0), (D, 0))),
    ]
    swapped = swap_pair(
        4,
        [pick(r, core) for r in lefts] + same + [pick_columns(grad_half, core)],
        [pick(r, 1 - core) for r in lefts] + same + [pick_columns(grad_half, 1 - core)],
    )
    norm_terms = jnp.stack([d_gain_one, d_gain_two, d_bias_one, d_bias_two])
    norm_terms = jnp.pad(norm_terms.reshape(4, 32, 34), ((0, 0), (0, 0), (0, 94)))
    ga, gb, gc = weight_grads(*swapped, norm_terms)
    fa, fb, fc = reduce_all(ga, gb, gc)
    full = jnp.concatenate(
        [fa.reshape(32, WIDE), fc[:, :, :17].reshape(2, WIDE)], axis=0
    ).astype(F32)
    full_second = jnp.concatenate(
        [fb[0], fb[1], edge_of(fc)], axis=1
    ).astype(F32)
    norm_sums = jnp.sum(fc[:, :, 17, :34].astype(F32), axis=0)
    return (
        resid_out.astype(BF),
        grad_tokens,
        norm_sums[None, :2],
        norm_sums[None, 2:],
        full[None, :, cols_qkv],
        full[None, :, cols_out],
        full[None, :, cols_first],
        full_second[None],
    )


def solution(mesh):
    rows = P(("rep", "fsdp"), None)
    last = P(None, None, "fsdp")
    middle = P(None, "fsdp", None)
    return jax.shard_map(
        body,
        mesh=mesh,
        in_specs=(rows, P(("rep", "fsdp")), last, last, middle, middle, middle, middle, rows),
        out_specs=(rows, rows, last, last, middle, middle, middle, middle),
        check_vma=False,
    )
```
